32 devices in a mesh: ctx: 16 (over z, y, x), head: 2 (over core).
Axes of the slice: x: 2, y: 2, z: 4, core: 2. Of those that a mesh axis runs over, the one named last changes fastest.
Arguments:
- queries: bfloat16 [2048, 8192], P('ctx', 'head'), may hold values from -6 to 6
- keys: bfloat16 [2048, 8192], P('ctx', 'head'), may hold values from -6 to 6
- values: bfloat16 [2048, 8192], P('ctx', 'head'), may hold values from -6 to 6
- log_decay: float32 [2048, 64], P('ctx', 'head'), may hold values from -1 to 0, as said below
- gain: float32 [8192], P('head'), may hold values from 0.1 to 1.9
- grad_out: bfloat16 [2048, 8192], P('ctx', 'head'), may hold values from -6 to 6
Outputs:
- normed: bfloat16 [2048, 8192], P('ctx', 'head')
- grad_queries: bfloat16 [2048, 8192], P('ctx', 'head')
- grad_keys: bfloat16 [2048, 8192], P('ctx', 'head')
- grad_values: bfloat16 [2048, 8192], P('ctx', 'head')
The draws below stay inside these ranges and needn't reach their ends.
Inputs may be any that keep to these rules, and one draw needn't show every extreme that they name: `log_decay`: entries are negative.
All inputs are finite; a program needn't handle non-finite values.
Results may differ from the reference program's by a relative error of at most 0.0095.
Values sent between devices are 32-bit elements; how exact they have to be, the bound alone decides.
No kernel may reach another device: no remote copies, remote signals or barrier semaphores. Data moves between devices by JAX's collectives and lax.ppermute only.
A program may use at most 128 MiB of HBM per device.

```python
import math
import jax
import jax.numpy as jnp
from jax import lax

HEADS = 64
HEAD_DIM = 128
TOK_DEV = 128
TOKEN_LENGTH = 2048
WIDTH = 8192
N_CTX = 16


def draw_log_decay(key, part):
    sequence_batch = jax.random.split(jax.random.fold_in(key, 7), 7)
    slow_rate = jax.random.uniform(sequence_batch[0], (HEADS,), jnp.float32, 0.05, 0.8) / TOKEN_LENGTH
    fast_rate = jnp.exp(jax.random.uniform(sequence_batch[1], (HEADS,), jnp.float32, math.log(1.0 / 50.0), math.log(1.0 / 25.0)))
    fast_share = 0.5
    is_fast = jax.random.uniform(sequence_batch[2], (HEADS,), jnp.float32) < fast_share
    baseline_decay_rate = jnp.where(is_fast, fast_rate, slow_rate)
    coarse_estimate = jnp.exp(jax.random.uniform(sequence_batch[3], (TOKEN_LENGTH, HEADS), jnp.float32, -0.7, 0.7))
    region_count = TOKEN_LENGTH // TOK_DEV
    region_factor = jnp.exp(jax.random.uniform(sequence_batch[4], (region_count, HEADS), jnp.float32, -0.7, 0.7))
    segment_rows = jnp.repeat(region_factor, TOK_DEV, axis=0)
    spike_location = jax.random.randint(sequence_batch[5], (2,), 0, TOKEN_LENGTH)
    spike_retention = jax.random.uniform(sequence_batch[6], (2,), jnp.float32, 0.5, 0.8)
    token_position = jnp.arange(TOKEN_LENGTH)
    spike_log_decay = jnp.sum(jnp.where(token_position[:, None] == spike_location[None, :], jnp.log(spike_retention)[None, :], 0.0), axis=1)
    return -baseline_decay_rate[None, :] * coarse_estimate * segment_rows + spike_log_decay[:, None]


def steps_of(rng, shape, cuts, least, largest):
    level, own = 1.0, jax.random.fold_in(rng, 6)
    for axis_at, shards_of in cuts:
        draws = jnp.exp(jax.random.uniform(jax.random.fold_in(own, axis_at), (shards_of,), jnp.float32, least / len(cuts), largest / len(cuts)))
        level = level * jnp.repeat(draws, shape[axis_at] // shards_of).reshape([-1 if axis == axis_at else 1 for axis in range(len(shape))])
    return level


def gaussian(own_key, shape, deviation, bound, pieces=(), held_as=jnp.bfloat16):
    loudness = steps_of(own_key, shape, pieces, -0.22, 0.18) if pieces else 1.0
    drawn = jax.random.normal(own_key, shape, jnp.float32) * deviation * loudness
    return jnp.minimum(jnp.maximum(drawn, -bound), bound).astype(held_as)


def setup_inputs(seed: int = 0) -> dict:
    key_of = jax.random.split(jax.random.key(seed), 7)
    queries = gaussian(key_of[0], (TOKEN_LENGTH, WIDTH), 1.0, 6.0, ((0, 16), (1, 2)))
    keys = gaussian(key_of[1], (TOKEN_LENGTH, WIDTH), 1.0, 6.0, ((0, 16), (1, 2)))
    values = gaussian(key_of[2], (TOKEN_LENGTH, WIDTH), 1.0, 6.0, ((0, 16), (1, 2)))
    log_decay = draw_log_decay(jax.random.fold_in(key_of[6], 71), 0)
    gain = jnp.clip(1.0 + 0.18 * jax.random.normal(key_of[4], (WIDTH,), jnp.float32), 0.1, 1.9)
    grad_out = gaussian(key_of[5], (TOKEN_LENGTH, WIDTH), 1.0, 6.0, ((0, 16), (1, 2)))
    return {"queries": queries, "keys": keys, "values": values, "log_decay": log_decay, "gain": gain, "grad_out": grad_out}


epsilon = 1e-06

def block_decays(log_block):
    cumulative = jnp.cumsum(log_block, axis=0)
    last_log = cumulative[-1]
    log_rows = cumulative.T
    spread = log_rows[:, :, None] - log_rows[:, None, :]
    count = log_block.shape[0]
    token_position = lax.broadcasted_iota(jnp.int32, (count, count), 0)
    source = lax.broadcasted_iota(jnp.int32, (count, count), 1)
    decay_matrix = jnp.where((token_position >= source)[None], jnp.exp(jnp.minimum(spread, 0.0)), 0.0)
    return (cumulative, last_log, decay_matrix)

def block_terms(query_block, key_block, value_block, log_block):
    cumulative, last_log, decay_matrix = block_decays(log_block)
    query_float = query_block.astype(jnp.float32)
    key_float = key_block.astype(jnp.float32)
    value_float = value_block.astype(jnp.float32)
    scores = jnp.einsum('thd,shd->hts', query_float, key_float)
    weights = lax.optimization_barrier((scores * decay_matrix).astype(jnp.bfloat16))
    intra_out = jnp.einsum('hts,shd->thd', weights.astype(jnp.float32), value_float)
    key_decay = jnp.exp(last_log[None, :] - cumulative)
    key_scaled = lax.optimization_barrier((key_decay[:, :, None] * key_float).astype(jnp.bfloat16))
    local_state = jnp.einsum('thd,the->hde', key_scaled.astype(jnp.float32), value_float, precision=lax.Precision.HIGHEST)
    query_decay = jnp.exp(cumulative)
    query_scaled = query_decay[:, :, None] * query_float
    return (weights, intra_out, key_decay, key_scaled, local_state, query_decay, query_scaled, jnp.exp(last_log), decay_matrix, query_float, key_float, value_float)

def reference(queries, keys, values, log_decay, gain, grad_out):
    shape_four = (N_CTX, TOK_DEV, HEADS, HEAD_DIM)
    query_blocks = queries.reshape(shape_four)
    key_blocks = keys.reshape(shape_four)
    value_blocks = values.reshape(shape_four)
    log_blocks = log_decay.reshape(N_CTX, TOK_DEV, HEADS)

    def forward_step(state, inputs):
        terms = block_terms(*inputs)
        inter_out = jnp.einsum('thd,hde->the', terms[6], state, precision=lax.Precision.HIGHEST)
        new_state = terms[7][:, None, None] * state + terms[4]
        return (new_state, (terms[1] + inter_out, state))
    start = jnp.zeros((HEADS, HEAD_DIM, HEAD_DIM), jnp.float32)
    _, (attended, entering) = lax.scan(forward_step, start, (query_blocks, key_blocks, value_blocks, log_blocks))
    attended = attended.reshape(TOKEN_LENGTH, HEADS * HEAD_DIM)
    total_width = HEADS * HEAD_DIM
    squares = lax.optimization_barrier(jnp.sum(attended * attended, axis=1))
    inverse = lax.rsqrt(squares / total_width + epsilon)
    normed = (attended * inverse[:, None] * gain[None, :]).astype(jnp.bfloat16)
    scaled_grad = grad_out.astype(jnp.float32) * gain[None, :]
    products = lax.optimization_barrier(jnp.sum(scaled_grad * attended, axis=1))
    grad_attended = (inverse[:, None] * scaled_grad - attended * (inverse ** 3 * products / total_width)[:, None]).astype(jnp.bfloat16)
    grad_blocks = grad_attended.reshape(shape_four)

    def backward_step(later, inputs):
        query_block, key_block, value_block, log_block, grad_block, entering_block = inputs
        weights, intra_out, key_decay, key_scaled, local_state, query_decay, query_scaled, block_decay, decay_matrix, query_float, key_float, value_float = block_terms(query_block, key_block, value_block, log_block)
        grad_float = grad_block.astype(jnp.float32)
        grad_state = jnp.einsum('thd,the->hde', query_scaled, grad_float, precision=lax.Precision.HIGHEST)
        grad_weights = jnp.einsum('the,she->hts', grad_float, value_float)
        grad_scores = lax.optimization_barrier((grad_weights * decay_matrix).astype(jnp.bfloat16)).astype(jnp.float32)
        grad_query = jnp.einsum('hts,shd->thd', grad_scores, key_float) + query_decay[:, :, None] * jnp.einsum('the,hde->thd', grad_float, entering_block, precision=lax.Precision.HIGHEST)
        grad_key = jnp.einsum('hts,thd->shd', grad_scores, query_float) + key_decay[:, :, None] * jnp.einsum('she,hde->shd', value_float, later, precision=lax.Precision.HIGHEST)
        grad_value = jnp.einsum('hts,thd->shd', weights.astype(jnp.float32), grad_float) + jnp.einsum('shd,hde->she', key_scaled.astype(jnp.float32), later, precision=lax.Precision.HIGHEST)
        new_later = grad_state + block_decay[:, None, None] * later
        return (new_later, (grad_query.astype(jnp.bfloat16), grad_key.astype(jnp.bfloat16), grad_value.astype(jnp.bfloat16)))
    _, (grad_q, grad_k, grad_v) = lax.scan(backward_step, start, (query_blocks, key_blocks, value_blocks, log_blocks, grad_blocks, entering), reverse=True)
    flat = (TOKEN_LENGTH, HEADS * HEAD_DIM)
    return (normed, grad_q.reshape(flat), grad_k.reshape(flat), grad_v.reshape(flat))
```

```python
import functools

import jax
import jax.numpy as jnp
from jax import lax
from jax.experimental import pallas as pl
from jax.experimental.pallas import tpu as pltpu
from jax.sharding import PartitionSpec as P

HEAD_DIM = 128
GROUP = 4
EPSILON = 1e-06
F32 = jnp.float32
BF16 = jnp.bfloat16
VMEM_LIMIT = 40 * 1024 * 1024


def dot(a, b, contract):
    return lax.dot_general(a, b, ((contract[:1], contract[1:]), ((), ())), preferred_element_type=F32)


def call(kernel, outs, ins, scratch=(), name=None):
    return pl.pallas_call(
        kernel,
        out_shape=outs,
        scratch_shapes=list(scratch),
        compiler_params=pltpu.CompilerParams(vmem_limit_bytes=VMEM_LIMIT),
        name=name,
    )(*ins)


class Plan:
    def __init__(self, rows, heads, width, ctx):
        self.rows, self.heads, self.width, self.ctx = rows, heads, width, ctx
        self.chunks = 2 if heads % (2 * GROUP) == 0 else 1
        self.chunk_heads = heads // self.chunks
        self.share = self.chunk_heads // GROUP
        self.planes = ctx // GROUP
        self.share_rows = self.share * width
        self.part_rows = self.share_rows // self.planes
        self.piece = min(self.part_rows, width)
        self.pieces = self.part_rows // self.piece
        self.tail = -(-self.share // 8) * 8
        self.part_tail = -(-self.pieces // 8) * 8
        self.chunk_width = self.chunk_heads * width

    def where(self):
        position = lax.axis_index("ctx")
        return lax.rem(position, GROUP), lax.div(position, GROUP)


def aligned(index, size):
    return pl.multiple_of(index, size)


def state_kernel(plan, chunk, first, decay_ref, key_ref, value_ref, *refs):
    if first:
        cum_ref, scaled_ref, *state_refs = refs
        spare = cum_ref.shape[1]
        rows = plan.rows
        lower = (
            lax.broadcasted_iota(jnp.int32, (rows, rows), 0)
            >= lax.broadcasted_iota(jnp.int32, (rows, rows), 1)
        ).astype(F32)
        cum_ref[...] = jnp.zeros((rows, spare), F32)
        cum_ref[:, : plan.heads] = lax.dot_general(
            lower,
            decay_ref[...],
            (((1,), (0,)), ((), ())),
            precision=lax.Precision.HIGHEST,
            preferred_element_type=F32,
        )
        cumulative = cum_ref[...]
    else:
        scaled_ref, *state_refs = refs
        cumulative = decay_ref[...]
    spare = cumulative.shape[1]
    mine, _ = plan.where()
    width = plan.width
    for slot in range(GROUP):
        quarter = jnp.bitwise_xor(mine, slot)
        head = chunk * plan.chunk_heads + quarter * plan.share
        turned = pltpu.roll(cumulative, lax.rem(spare - head, spare), 1)
        last = turned[plan.rows - 1 :, :]
        key_decay = jnp.exp(last - turned)
        state_refs[slot][plan.share_rows :, :] = jnp.zeros((plan.tail, width), F32)
        for i in range(plan.share):
            at = pl.ds(aligned(quarter * plan.share_rows + i * width, width), width)
            key = key_ref[:, pl.ds(aligned((head + i) * width, width), width)].astype(F32)
            value = value_ref[:, pl.ds(aligned((head + i) * width, width), width)]
            scaled = (key_decay[:, i : i + 1] * key).astype(BF16)
            scaled_ref[:, at] = scaled
            state_refs[slot][i * width : (i + 1) * width, :] = dot(scaled, value, (0, 0))
            state_refs[slot][plan.share_rows + i : plan.share_rows + i + 1, :] = jnp.broadcast_to(
                last[:, i : i + 1], (1, width)
            )


def intra_kernel(plan, cum_ref, query_ref, key_ref, value_ref, weight_ref, decay_ref, intra_ref, scaled_ref):
    rows, width = plan.rows, plan.width
    cumulative = cum_ref[...]
    across = cumulative.T
    lower = lax.broadcasted_iota(jnp.int32, (rows, rows), 0) >= lax.broadcasted_iota(
        jnp.int32, (rows, rows), 1
    )
    query_decay = jnp.exp(cumulative)
    for h in range(plan.heads):
        at = slice(h * width, (h + 1) * width)
        spread = jnp.minimum(cumulative[:, h : h + 1] - across[h : h + 1, :], 0.0)
        decay = jnp.where(lower, jnp.exp(spread), 0.0)
        query = query_ref[:, at]
        weights = (dot(query, key_ref[:, at], (1, 1)) * decay).astype(BF16)
        weight_ref[h] = weights
        decay_ref[h] = decay
        intra_ref[:, at] = dot(weights, value_ref[:, at], (1, 0))
        scaled_ref[:, at] = (query_decay[:, h : h + 1] * query.astype(F32)).astype(BF16)


def between(logs, ranks, low, high):
    total = jnp.zeros_like(logs[0])
    for log, rank in zip(logs, ranks):
        inside = jnp.logical_and(rank > low, rank < high)
        total = total + jnp.where(inside, log, 0.0)
    return jnp.exp(total)


def group_ranks(mine, reverse):
    ranks = [jnp.bitwise_xor(mine, slot) for slot in range(GROUP)]
    return [GROUP - 1 - r for r in ranks] if reverse else ranks


def total_kernel(plan, reverse, *refs):
    share_refs, refs = refs[:GROUP], refs[GROUP:]
    if reverse:
        log_ref, part_refs = refs[0], refs[1:]
    else:
        log_ref, part_refs = refs[0], refs[1:]
        for slot in range(GROUP):
            log_ref[slot] = share_refs[slot][plan.share_rows :, :]
    mine, plane = plan.where()
    ranks = group_ranks(mine, reverse)
    for slot in range(plan.planes):
        part = lax.rem(plane + slot, plan.planes)
        if not reverse:
            part_refs[slot][plan.part_rows :, :] = jnp.zeros((plan.part_tail, plan.width), F32)
        for i in range(plan.pieces):
            start = part * plan.part_rows + i * plan.piece
            head = lax.div(start, plan.width)
            logs = [log_ref[s, pl.ds(head, 1), :] for s in range(GROUP)]
            total = jnp.zeros((plan.piece, plan.width), F32)
            for s in range(GROUP):
                factor = between(logs, ranks, ranks[s], GROUP)
                total = total + factor * share_refs[s][pl.ds(aligned(start, plan.piece), plan.piece), :]
            part_refs[slot][i * plan.piece : (i + 1) * plan.piece, :] = total
            if not reverse:
                part_refs[slot][plan.part_rows + i : plan.part_rows + i + 1, :] = sum(logs)


def plane_kernel(plan, reverse, *refs):
    count = plan.planes
    total_refs, refs = refs[:count], refs[count:]
    log_ref, out_refs = refs[0], refs[1:]
    if not reverse:
        for slot in range(count):
            log_ref[slot] = total_refs[slot][plan.part_rows :, :]
    _, plane = plan.where()
    sources = [lax.rem(plane - slot + count, count) for slot in range(count)]
    targets = [lax.rem(plane + slot, count) for slot in range(count)]
    if reverse:
        sources = [count - 1 - s for s in sources]
        targets = [count - 1 - t for t in targets]
    for i in range(plan.pieces):
        at = slice(i * plan.piece, (i + 1) * plan.piece)
        logs = [log_ref[s, i : i + 1, :] for s in range(count)]
        for t in range(count):
            total = jnp.zeros((plan.piece, plan.width), F32)
            for s in range(count):
                factor = between(logs, sources, sources[s], targets[t])
                factor = jnp.where(sources[s] < targets[t], factor, 0.0)
                total = total + factor * total_refs[s][at, :]
            out_refs[t][at, :] = total


def enter_kernel(plan, reverse, *refs):
    count = plan.planes
    before_refs, refs = refs[:count], refs[count:]
    share_refs, refs = refs[:GROUP], refs[GROUP:]
    log_ref, out_refs = refs[0], refs[1:]
    mine, plane = plan.where()
    ranks = group_ranks(mine, reverse)
    for slot in range(count):
        part = lax.rem(plane - slot + count, count)
        for i in range(plan.pieces):
            start = part * plan.part_rows + i * plan.piece
            head = lax.div(start, plan.width)
            at = pl.ds(aligned(start, plan.piece), plan.piece)
            logs = [log_ref[s, pl.ds(head, 1), :] for s in range(GROUP)]
            before = before_refs[slot][i * plan.piece : (i + 1) * plan.piece, :]
            shares = [share_refs[s][at, :] for s in range(GROUP)]
            for t in range(GROUP):
                total = between(logs, ranks, -1, ranks[t]) * before
                for s in range(GROUP):
                    if s != t:
                        factor = between(logs, ranks, ranks[s], ranks[t])
                        total = total + jnp.where(ranks[s] < ranks[t], factor, 0.0) * shares[s]
                out_refs[t][at, :] = total


def attend_kernel(plan, chunk, scaled_ref, intra_ref, grad_ref, gain_ref, *refs):
    enter_refs, refs = refs[:GROUP], refs[GROUP:]
    if chunk:
        before_ref, refs = refs[0], refs[1:]
    out_ref, sum_ref = refs
    mine, _ = plan.where()
    rows, width = plan.rows, plan.width
    squares = jnp.zeros((rows, width), F32)
    products = jnp.zeros((rows, width), F32)
    for slot in range(GROUP):
        quarter = jnp.bitwise_xor(mine, slot)
        for i in range(plan.share):
            local = aligned(quarter * plan.share_rows + i * width, width)
            at = pl.ds(aligned(chunk * plan.chunk_width + local, width), width)
            entering = enter_refs[slot][i * width : (i + 1) * width, :].astype(BF16)
            attended = intra_ref[:, at] + dot(scaled_ref[:, at], entering, (1, 0))
            out_ref[:, pl.ds(local, width)] = attended
            scaled_grad = grad_ref[:, at].astype(F32) * gain_ref[:, at]
            squares = squares + attended * attended
            products = products + scaled_grad * attended
    squares = jnp.sum(squares, axis=1, keepdims=True)
    products = jnp.sum(products, axis=1, keepdims=True)
    lane = lax.broadcasted_iota(jnp.int32, (rows, width), 1)
    sums = jnp.where(lane == 0, squares, jnp.where(lane == 1, products, 0.0))
    if chunk:
        sums = sums + before_ref[...]
    sum_ref[...] = sums


def row_factors(total_width, sums):
    inverse = lax.rsqrt(sums[:, 0:1] / total_width + EPSILON)
    return inverse, inverse * inverse * inverse * sums[:, 1:2] / total_width


def grad_kernel(plan, chunk, total_width, attended_ref, sum_ref, grad_ref, gain_ref, scaled_ref, *refs):
    out_ref, *state_refs = refs
    mine, _ = plan.where()
    width = plan.width
    inverse, pull = row_factors(total_width, sum_ref[...])
    inverse = jnp.broadcast_to(inverse, (plan.rows, width))
    pull = jnp.broadcast_to(pull, (plan.rows, width))
    for slot in range(GROUP):
        quarter = jnp.bitwise_xor(mine, slot)
        for i in range(plan.share):
            local = aligned(quarter * plan.share_rows + i * width, width)
            at = pl.ds(aligned(chunk * plan.chunk_width + local, width), width)
            scaled_grad = grad_ref[:, at].astype(F32) * gain_ref[:, at]
            attended = attended_ref[:, pl.ds(local, width)]
            grad = (inverse * scaled_grad - attended * pull).astype(BF16)
            out_ref[:, pl.ds(local, width)] = grad
            state_refs[slot][i * width : (i + 1) * width, :] = dot(scaled_ref[:, at], grad, (0, 0))


def inner_kernel(plan, total_width, *refs):
    chunks = plan.chunks
    attended_refs, refs = refs[:chunks], refs[chunks:]
    grad_refs, refs = refs[:chunks], refs[chunks:]
    enter_refs, refs = refs[: chunks * GROUP], refs[chunks * GROUP :]
    sum_ref, gain_ref, cum_ref, query_ref, key_ref, value_ref, weight_ref, decay_ref, *refs = refs
    normed_ref, query_out, key_out, value_out = refs
    mine, _ = plan.where()
    width = plan.width
    inverse, _ = row_factors(total_width, sum_ref[...])
    inverse = jnp.broadcast_to(inverse, (plan.rows, width))
    cumulative = cum_ref[...]
    spare = cumulative.shape[1]
    for chunk in range(chunks):
        for slot in range(GROUP):
            quarter = jnp.bitwise_xor(mine, slot)
            first = chunk * plan.chunk_heads + quarter * plan.share
            query_decay = jnp.exp(pltpu.roll(cumulative, lax.rem(spare - first, spare), 1))
            for i in range(plan.share):
                head = first + i
                local = pl.ds(aligned(quarter * plan.share_rows + i * width, width), width)
                at = pl.ds(aligned(head * width, width), width)
                attended = attended_refs[chunk][:, local]
                normed_ref[:, at] = (attended * inverse * gain_ref[:, at]).astype(BF16)
                grad = grad_refs[chunk][:, local]
                scores = (dot(grad, value_ref[:, at], (1, 1)) * decay_ref[head]).astype(BF16)
                entering = enter_refs[chunk * GROUP + slot][i * width : (i + 1) * width, :].astype(BF16)
                inter = dot(grad, entering, (1, 1))
                query_out[:, at] = (
                    dot(scores, key_ref[:, at], (1, 0)) + query_decay[:, i : i + 1] * inter
                ).astype(BF16)
                key_out[:, at] = dot(scores, query_ref[:, at], (0, 0))
                value_out[:, at] = dot(weight_ref[head], grad, (0, 0))


def outer_kernel(plan, chunk, cum_ref, value_ref, scaled_ref, key_in, value_in, *refs):
    later_refs, refs = refs[:GROUP], refs[GROUP:]
    before, (key_out, value_out) = refs[:-2], refs[-2:]
    mine, _ = plan.where()
    width = plan.width
    cumulative = cum_ref[...]
    spare = cumulative.shape[1]
    base = 0
    if chunk == plan.chunks - 1:
        for c in range(chunk):
            done = slice(c * plan.chunk_width, (c + 1) * plan.chunk_width)
            key_out[:, done] = before[2 * c][...]
            value_out[:, done] = before[2 * c + 1][...]
        base = chunk * plan.chunk_width
    for slot in range(GROUP):
        quarter = jnp.bitwise_xor(mine, slot)
        head = chunk * plan.chunk_heads + quarter * plan.share
        turned = pltpu.roll(cumulative, lax.rem(spare - head, spare), 1)
        key_decay = jnp.exp(turned[plan.rows - 1 :, :] - turned)
        for i in range(plan.share):
            local = aligned(quarter * plan.share_rows + i * width, width)
            at = pl.ds(aligned(chunk * plan.chunk_width + local, width), width)
            to = pl.ds(aligned(base + local, width), width)
            later = later_refs[slot][i * width : (i + 1) * width, :].astype(BF16)
            inter = dot(value_ref[:, at], later, (1, 1))
            key_out[:, to] = (key_in[:, at] + key_decay[:, i : i + 1] * inter).astype(BF16)
            value_out[:, to] = (
                value_in[:, at] + dot(scaled_ref[:, pl.ds(local, width)], later, (1, 0))
            ).astype(BF16)


def exchange(plan, slots):
    pairs = lambda s: [(c, c ^ s) for c in range(plan.ctx)]
    return [slots[0]] + [lax.ppermute(slots[s], "ctx", pairs(s)) for s in range(1, GROUP)]


def shift(plan, slots):
    pairs = lambda s: [(c, (c + GROUP * s) % plan.ctx) for c in range(plan.ctx)]
    return [slots[0]] + [lax.ppermute(slots[s], "ctx", pairs(s)) for s in range(1, plan.planes)]


def scan(plan, slots, logs=None):
    reverse = logs is not None
    side = "later" if reverse else "enter"
    shape = lambda *s: jax.ShapeDtypeStruct(s, F32)
    width, tail, part_tail = plan.width, plan.tail, plan.part_tail
    shares = exchange(plan, slots)
    parts = [shape(plan.part_rows + (0 if reverse else part_tail), width)] * plan.planes
    total = functools.partial(total_kernel, plan, reverse)
    if reverse:
        group_logs, plane_logs = logs
        parts = call(total, parts, (*shares, group_logs), name=side + "_total")
    else:
        group_logs, *parts = call(
            total, [shape(GROUP, tail, width)] + parts, shares, name=side + "_total"
        )
    totals = shift(plan, parts)
    outs = [shape(plan.part_rows, width)] * plan.planes
    plane = functools.partial(plane_kernel, plan, reverse)
    if reverse:
        befores = call(plane, outs, (*totals, plane_logs), name=side + "_plane")
    else:
        plane_logs, *befores = call(
            plane, [shape(plan.planes, part_tail, width)] + outs, totals, name=side + "_plane"
        )
    befores = shift(plan, befores)
    outs = call(
        functools.partial(enter_kernel, plan, reverse),
        [shape(plan.share_rows, width)] * GROUP,
        (*befores, *shares, group_logs),
        name=side + "_combine",
    )
    return exchange(plan, outs), (group_logs, plane_logs)


def head_sum(array):
    if lax.axis_size("head") == 2:
        return array + lax.ppermute(array, "head", [(0, 1), (1, 0)])
    return lax.psum(array, "head")


def body(queries, keys, values, log_decay, gain, grad_out):
    rows, heads = log_decay.shape
    features = queries.shape[1]
    plan = Plan(rows, heads, features // heads, lax.axis_size("ctx"))
    total_width = features * lax.axis_size("head")
    shape = jax.ShapeDtypeStruct
    lanes = -(-heads // 128) * 128
    gain = gain[None, :]
    chunks = range(plan.chunks)

    cumulative, scaled_keys, entering, logs = None, [], [], []
    for c in chunks:
        outs = [shape((rows, plan.chunk_width), BF16)]
        outs += [shape((plan.share_rows + plan.tail, plan.width), F32)] * GROUP
        kernel = functools.partial(state_kernel, plan, c, c == 0)
        if c == 0:
            cumulative, scaled, *states = call(
                kernel, [shape((rows, lanes), F32)] + outs, (log_decay, keys, values), name="state"
            )
        else:
            scaled, *states = call(kernel, outs, (cumulative, keys, values), name="state")
        scaled_keys.append(scaled)
        entered, log = scan(plan, states)
        entering.append(entered)
        logs.append(log)

    weights, decays, intra, scaled_queries = call(
        functools.partial(intra_kernel, plan),
        [
            shape((heads, rows, rows), BF16),
            shape((heads, rows, rows), F32),
            shape((rows, features), F32),
            shape((rows, features), BF16),
        ],
        (cumulative, queries, keys, values),
        name="intra",
    )

    attended, sums = [], None
    for c in chunks:
        out, sums = call(
            functools.partial(attend_kernel, plan, c),
            [shape((rows, plan.chunk_width), F32), shape((rows, plan.width), F32)],
            (scaled_queries, intra, grad_out, gain, *entering[c]) + ((sums,) if c else ()),
            name="attend",
        )
        attended.append(out)
    sums = head_sum(sums)

    grads, later = [], []
    for c in chunks:
        grad, *states = call(
            functools.partial(grad_kernel, plan, c, total_width),
            [shape((rows, plan.chunk_width), BF16)]
            + [shape((plan.share_rows, plan.width), F32)] * GROUP,
            (attended[c], sums, grad_out, gain, scaled_queries),
            name="grad",
        )
        grads.append(grad)
        later.append(scan(plan, states, logs[c])[0])

    normed, grad_queries, key_inner, value_inner = call(
        functools.partial(inner_kernel, plan, total_width),
        [shape((rows, features), BF16)] * 2 + [shape((rows, features), F32)] * 2,
        (*attended, *grads, *sum(entering, []), sums, gain, cumulative)
        + (queries, keys, values, weights, decays),
        name="inner",
    )

    before = []
    for c in chunks:
        size = features if c == plan.chunks - 1 else plan.chunk_width
        before += call(
            functools.partial(outer_kernel, plan, c),
            [shape((rows, size), BF16)] * 2,
            (cumulative, values, scaled_keys[c], key_inner, value_inner, *later[c])
            + (tuple(before) if c == plan.chunks - 1 else ()),
            name="outer",
        )
    return normed, grad_queries, before[-2], before[-1]


def solution(mesh):
    split = P("ctx", "head")
    return jax.shard_map(
        body,
        mesh=mesh,
        in_specs=(split, split, split, split, P("head"), split),
        out_specs=(split, split, split, split),
        check_vma=False,
    )
```
